256 devices in a mesh: op: 32 (over x, z_hi, core), sec: 8 (over y, z_lo).
Axes of the slice: x: 4, y: 4, z: 8 (z_hi: 4, z_lo: 2; z = z_hi * 2 + z_lo), core: 2. Of those that a mesh axis runs over, the one named last changes fastest.
Arguments:
- left_ops: float32 [32, 8, 1024, 1024], P('op', 'sec'), may hold values from -0.5 to 3.5
- right_ops: float32 [32, 8, 1024, 1024], P('op', 'sec'), may hold values from -0.5 to 3.5
- amplitudes: float32 [8, 1024, 1024], P('sec', 'op'), may hold values from -72 to 72
- sketch: float32 [1024, 512], replicated, may hold values from -0.1875 to 0.1875
- sector_shift: int32 [32], P('op'), may hold values from 0 to 3
Outputs:
- rotated: float32 [32, 8, 512, 512], P('op', 'sec')
- new_basis: float32 [8, 1024, 512], P('sec', 'op')
- energy: float32 [], replicated
The draws below stay inside these ranges and needn't reach their ends.
Inputs may be any that keep to these rules, and one draw needn't show every extreme that they name: The target sector of pair k from source sector s is (s + sector_shift[k]) mod 8.
All inputs are finite; a program needn't handle non-finite values.
Results may differ from the reference program's by a relative error of at most 0.0003.
Values sent between devices are 32-bit elements; how exact they have to be, the bound alone decides.
No kernel may reach another device: no remote copies, remote signals or barrier semaphores. Data moves between devices by JAX's collectives and lax.ppermute only.
A program may use at most 128 MiB of HBM per device.

```python
import jax
import jax.numpy as jnp
from jax import lax

M = 1024
KEEP = 512
PAIRS = 32
SECTORS = 8


def dominant(key):
    key_diag, key_rest = jax.random.split(key)
    jitter = jnp.clip(jax.random.normal(key_rest, (PAIRS, SECTORS, M, M), jnp.float32), -6.0, 6.0)
    diagonal = 10.0 ** jax.random.uniform(key_diag, (PAIRS, SECTORS, M, 1), jnp.float32, -0.3, 0.3)
    identity = jnp.eye(M, dtype=jnp.float32)
    return jitter * (0.5 * M ** (-0.5)) + identity * diagonal


def draw_left_ops(key, part):
    return dominant(jax.random.fold_in(key, 101))


def draw_right_ops(key, part):
    return dominant(jax.random.fold_in(key, 202))


def draw_amplitudes(key, part):
    key_jitter, key_rows, key_cols = jax.random.split(jax.random.fold_in(key, 303), 3)
    jitter = jnp.clip(jax.random.normal(key_jitter, (SECTORS, M, M), jnp.float32), -6.0, 6.0)
    rising = 10.0 ** (jnp.arange(M, dtype=jnp.float32) / M)
    row_rough = jax.random.uniform(key_rows, (SECTORS, M, 1), jnp.float32, 0.5, 1.5)
    col_scale = 10.0 ** jax.random.uniform(key_cols, (SECTORS, 1, M), jnp.float32, 0.0, 0.5)
    return jitter * rising[None, :, None] * row_rough * col_scale / 4.0


def with_ends(result, key, low, largest):
    longest = result.shape.index(max(result.shape))
    spots = []
    for shift in (0, 1):
        where = [jax.random.randint(jax.random.fold_in(key, axis), (), 0, length) for axis, length in enumerate(result.shape)]
        where[longest] = (where[longest] + shift) % result.shape[longest]
        spots.append(tuple(where))
    return result.at[spots[0]].set(low).at[spots[1]].set(largest)


def centred(own_key, extent, scale, limit, kind=jnp.bfloat16):
    entries = jax.random.normal(own_key, extent, jnp.float32) * scale
    return jnp.minimum(jnp.maximum(entries, -limit), limit).astype(kind)


def setup_inputs(seed: int = 0) -> dict:
    arg_keys = jax.random.split(jax.random.key(seed), 6)
    return {
        "left_ops": draw_left_ops(jax.random.fold_in(arg_keys[5], 71), 0),
        "right_ops": draw_right_ops(jax.random.fold_in(arg_keys[5], 71), 0),
        "amplitudes": draw_amplitudes(jax.random.fold_in(arg_keys[5], 71), 0),
        "sketch": centred(arg_keys[3], (M, KEEP), M ** -0.5, 0.1875, jnp.float32),
        "sector_shift": with_ends(jax.random.randint(arg_keys[4], (PAIRS,), 0, 4), jax.random.fold_in(arg_keys[4], 1), 0, 3).astype(jnp.int32),
    }


EXACT = lax.Precision.HIGHEST

def solve_one(factor_one, sketch_one):
    return jax.scipy.linalg.solve_triangular(factor_one, sketch_one.T, lower=True).T

def reference(left_ops, right_ops, amplitudes, sketch, sector_shift):

    def add_pair(running, inputs):
        left_pair, right_pair, offset = inputs

        def per_sector(sector):
            right_part = jnp.dot(amplitudes[sector].astype(jnp.float32), right_pair[sector].astype(jnp.float32), precision=EXACT, preferred_element_type=jnp.float32)
            return jnp.dot(left_pair[sector].astype(jnp.float32), right_part.astype(jnp.float32), precision=EXACT, preferred_element_type=jnp.float32)
        sector_terms = lax.map(per_sector, jnp.arange(SECTORS, dtype=jnp.int32))
        return (running + jnp.roll(sector_terms, offset, axis=0), None)
    product, unused_out = lax.scan(add_pair, jnp.zeros_like(amplitudes), (left_ops, right_ops, sector_shift))
    correlation = jnp.sum(amplitudes * product)
    norm_sq = jnp.sum(amplitudes * amplitudes)
    energy = correlation / norm_sq
    residual = product - energy * amplitudes
    sketched = jnp.einsum('smn,nk->smk', residual, sketch, precision=EXACT)
    gram_mat = jnp.einsum('smk,sml->skl', sketched, sketched, precision=EXACT)
    factor = jnp.linalg.cholesky(gram_mat)
    new_basis = jax.vmap(solve_one)(factor, sketched)

    def rotate(carried, inputs):
        left_pair, offset = inputs
        applied = jnp.einsum('smn,snk->smk', left_pair, new_basis, precision=EXACT)
        target = jnp.roll(new_basis, -offset, axis=0)
        return (carried, jnp.einsum('smk,sml->skl', target, applied, precision=EXACT))
    carried_out, rotated = lax.scan(rotate, jnp.zeros((), jnp.float32), (left_ops, sector_shift))
    return (rotated, new_basis, energy)
```

```python
import jax
import jax.numpy as jnp
from jax import lax
from jax.experimental import pallas as pl
from jax.experimental.pallas import tpu as pltpu
from jax.sharding import Mesh
from jax.sharding import PartitionSpec as P

OP = ("op_0", "op_1", "op_2")
SEC = ("sec_0", "sec_1")
OP_SEC = ("op_0", "op_1", "op_2", "sec_0", "sec_1")
CLASSES = 4
NB = 128
STEP = 8
EXACT = lax.Precision.HIGHEST
CLOSE = lax.Precision.HIGH


def dot(first, second, dims, precision=EXACT):
    return lax.dot_general(first, second, (dims, ((), ())), precision=precision, preferred_element_type=jnp.float32)


def matmul(first, second, precision=EXACT):
    return dot(first, second, ((1,), (0,)), precision)


def contract_rows(first, second, precision=EXACT):
    return dot(first, second, ((0,), (0,)), precision)


def contract_cols(first, second, precision=EXACT):
    return dot(first, second, ((1,), (1,)), precision)


def unit_factor(block, step):
    sub = lax.broadcasted_iota(jnp.int32, (8, NB), 0)
    lane = lax.broadcasted_iota(jnp.int32, (8, NB), 1)
    rows = [block[8 * r : 8 * r + 8] for r in range(NB // 8)]
    for start in range(0, NB, step):
        live = range(start // 8, NB // 8)
        cols = [{r: jnp.broadcast_to(rows[r][:, start + q : start + q + 1], (8, NB)) for r in live} for q in range(step)]
        for q in range(step):
            j = start + q
            at, inside = divmod(j, 8)
            one = slice(inside, inside + 1)
            inv = 1.0 / cols[q][at][one]
            line = jnp.broadcast_to(jnp.where(lane[:1] == j, 1.0, rows[at][one]) * inv, (8, NB))
            later = {p: jnp.broadcast_to(cols[p][at][one] * inv, (8, NB)) for p in range(q + 1, step)}
            for r in range(at, NB // 8):
                factor = cols[q][r]
                hit = lane == j
                if r == at:
                    factor = jnp.where(sub > inside, factor, 0.0)
                    hit = hit & (sub > inside)
                rows[r] = jnp.where(hit, 0.0, rows[r]) - factor * line
                for p in later:
                    cols[p][r] = cols[p][r] - factor * later[p]
    return jnp.concatenate(rows, axis=0)


def inverse_factor_kernel(gram, out, work, low):
    n = gram.shape[0]
    work[...] = gram[...]
    low[...] = jnp.zeros_like(low)
    out[...] = jnp.zeros_like(out)
    row = lax.broadcasted_iota(jnp.int32, (NB, NB), 0)
    col = lax.broadcasted_iota(jnp.int32, (NB, NB), 1)

    def panel(p, carried):
        at = pl.ds(pl.multiple_of(p * NB, NB), NB)
        done = unit_factor(work[at, at], STEP)
        pivots = jnp.sum(jnp.where(row == col, done, 0.0), axis=1, keepdims=True)
        unit = jnp.where(row > col, done, jnp.where(row == col, 1.0, 0.0))
        inv = unit * (1.0 / jnp.sqrt(pivots))
        below = lax.broadcasted_iota(jnp.int32, (n, NB), 0) >= (p + 1) * NB
        panel_col = jnp.where(below, contract_cols(work[:, at], inv), 0.0)
        work[...] = work[...] - contract_cols(panel_col, panel_col)
        out[at, :] = -matmul(inv, matmul(low[at, :], out[...]))
        out[at, at] = inv
        low[:, at] = panel_col
        return carried

    lax.fori_loop(0, n // NB, panel, 0)


def inverse_factor(gram):
    in_vmem = pl.BlockSpec(memory_space=pltpu.VMEM)
    return pl.pallas_call(
        inverse_factor_kernel,
        out_shape=jax.ShapeDtypeStruct(gram.shape, jnp.float32),
        in_specs=[in_vmem],
        out_specs=in_vmem,
        scratch_shapes=[pltpu.VMEM(gram.shape, jnp.float32)] * 2,
        name="inverse_factor",
    )(gram)


def class_sums_kernel(shifts, blocks, out):
    k = pl.program_id(0)

    @pl.when(k == 0)
    def _():
        out[...] = jnp.zeros_like(out)

    for i in range(blocks.shape[0]):
        c = shifts[k * blocks.shape[0] + i]
        out[c] = out[c] + blocks[i]


def class_sums(blocks, shifts):
    count, rows, width = blocks.shape
    per = 4
    return pl.pallas_call(
        class_sums_kernel,
        out_shape=jax.ShapeDtypeStruct((CLASSES, rows, width), jnp.float32),
        grid=(count // per,),
        in_specs=[pl.BlockSpec(memory_space=pltpu.SMEM), pl.BlockSpec((per, rows, width), lambda k: (k, 0, 0))],
        out_specs=pl.BlockSpec((CLASSES, rows, width), lambda k: (0, 0, 0)),
        name="class_sums",
    )(shifts, blocks)


def shifted(block, axis, distance):
    length = lax.axis_size(axis)
    return lax.ppermute(block, axis, [((i - distance) % length, i) for i in range(length)])


def sent_to_all(x, axis):
    length = lax.axis_size(axis)
    return lax.all_to_all(jnp.broadcast_to(x[None], (length, *x.shape)), axis, 0, 0, tiled=True)


def stacked_over(x, axis, dim):
    length = lax.axis_size(axis)
    here = lax.axis_index(axis)
    arrived = [x] + [shifted(x, axis, d) for d in range(1, length)]
    whole = jnp.zeros((*x.shape[:dim], length, *x.shape[dim:]), x.dtype)
    for d in range(length):
        whole = lax.dynamic_update_index_in_dim(whole, arrived[d], (here - d) % length, dim)
    return whole


def gathered_rows(x):
    whole = stacked_over(stacked_over(stacked_over(x, "op_1", 0), "op_0", 0), "op_2", 2)
    return whole.reshape(-1, x.shape[-1])


TRI = [(i, j) for i in range(4) for j in range(i + 1)]


def packed(low):
    return jnp.stack([low[i * NB : i * NB + NB, j * NB : j * NB + NB] for i, j in TRI])


def unpacked(blocks):
    blank = jnp.zeros((NB, NB), jnp.float32)
    rows = [[blocks[TRI.index((i, j))] if j <= i else blank for j in range(4)] for i in range(4)]
    return jnp.concatenate([jnp.concatenate(r, axis=1) for r in rows], axis=0)


def from_target(x, offset):
    for bit in range(2):
        arrived = shifted(x, SEC, -(1 << bit))
        x = jnp.where((offset >> bit) % 2 == 1, arrived, x)
    return x


def body(left_ops, right_ops, amplitudes, sketch, sector_shift):
    left_op = left_ops[0, 0]
    right_op = right_ops[0, 0]
    state_slab = amplitudes[0]
    offset = sector_shift[0]
    shifts = sent_to_all(jnp.broadcast_to(sector_shift.astype(jnp.float32)[:, None], (1, 128)), OP)[:, 0, 0].astype(jnp.int32)
    term = matmul(left_op, matmul(gathered_rows(state_slab), right_op))
    blocks = lax.all_to_all(term.reshape(32, -1, term.shape[-1]), OP, 0, 0, tiled=True)
    class_parts = class_sums(blocks, shifts)
    product_slab = class_parts[0] + shifted(class_parts[1], SEC, 1) + shifted(class_parts[2], SEC, 2) + shifted(class_parts[3], SEC, 3)
    partial = jnp.stack([jnp.sum(state_slab * product_slab), jnp.sum(state_slab * state_slab)])
    totals = jnp.sum(sent_to_all(jnp.pad(partial, (0, 126))[None], OP_SEC), axis=(0, 1))
    energy = totals[0] / totals[1]
    sketched = matmul(product_slab - energy * state_slab, sketch)
    candidates = sketched[None]
    for bit in range(2):
        candidates = jnp.concatenate([candidates, shifted(candidates, SEC, -(1 << bit))], axis=0)
    all_full = lax.all_gather(candidates, OP, axis=1, tiled=True)
    own_full = gathered_rows(sketched)
    inverse = inverse_factor(contract_rows(own_full, own_full))
    basis_slab = contract_cols(sketched, inverse)
    target_inverse = unpacked(from_target(packed(inverse), offset))
    applied = matmul(left_op, contract_cols(own_full, inverse, CLOSE), CLOSE)
    target = lax.dynamic_index_in_dim(all_full, offset, 0, keepdims=False)
    rotated = matmul(target_inverse, contract_rows(target, applied, CLOSE), CLOSE)
    return (rotated[None, None], basis_slab[None], energy)


def solution(mesh):
    split = Mesh(mesh.devices.reshape(4, 4, 2, 4, 2), ("op_0", "op_1", "op_2", "sec_0", "sec_1"))
    in_specs = (P(OP, SEC, None, None), P(OP, SEC, None, None), P(SEC, OP, None), P(), P(OP))
    out_specs = (P(OP, SEC, None, None), P(SEC, OP, None), P())
    return jax.shard_map(body, mesh=split, in_specs=in_specs, out_specs=out_specs, check_vma=False)
```

```python
import jax
import jax.numpy as jnp
from jax import lax
from jax.experimental import pallas as pl
from jax.experimental.pallas import tpu as pltpu
from jax.sharding import Mesh
from jax.sharding import PartitionSpec as P

OP = ("op_0", "op_1", "op_2")
SEC = ("sec_0", "sec_1")
OP_SEC = ("op_0", "op_1", "op_2", "sec_0", "sec_1")
CLASSES = 4
NB = 128
STEP = 8
TRI = [(i, j) for i in range(4) for j in range(i + 1)]
EXACT = lax.Precision.HIGHEST
CLOSE = lax.Precision.HIGH


def dot(first, second, dims, precision=EXACT):
    return lax.dot_general(first, second, (dims, ((), ())), precision=precision, preferred_element_type=jnp.float32)


def matmul(first, second, precision=EXACT):
    return dot(first, second, ((1,), (0,)), precision)


def contract_rows(first, second, precision=EXACT):
    return dot(first, second, ((0,), (0,)), precision)


def contract_cols(first, second, precision=EXACT):
    return dot(first, second, ((1,), (1,)), precision)


def unit_factor(block, step):
    sub = lax.broadcasted_iota(jnp.int32, (8, NB), 0)
    lane = lax.broadcasted_iota(jnp.int32, (8, NB), 1)
    rows = [block[8 * r : 8 * r + 8] for r in range(NB // 8)]
    for start in range(0, NB, step):
        live = range(start // 8, NB // 8)
        cols = [{r: jnp.broadcast_to(rows[r][:, start + q : start + q + 1], (8, NB)) for r in live} for q in range(step)]
        for q in range(step):
            j = start + q
            at, inside = divmod(j, 8)
            one = slice(inside, inside + 1)
            inv = 1.0 / cols[q][at][one]
            line = jnp.broadcast_to(jnp.where(lane[:1] == j, 1.0, rows[at][one]) * inv, (8, NB))
            later = {p: jnp.broadcast_to(cols[p][at][one] * inv, (8, NB)) for p in range(q + 1, step)}
            for r in range(at, NB // 8):
                factor = cols[q][r]
                hit = lane == j
                if r == at:
                    factor = jnp.where(sub > inside, factor, 0.0)
                    hit = hit & (sub > inside)
                rows[r] = jnp.where(hit, 0.0, rows[r]) - factor * line
                for p in later:
                    cols[p][r] = cols[p][r] - factor * later[p]
    return jnp.concatenate(rows, axis=0)


def inverse_factor_kernel(gram, out, packed, work, low):
    n = gram.shape[0]
    work[...] = gram[...]
    low[...] = jnp.zeros_like(low)
    out[...] = jnp.zeros_like(out)
    row = lax.broadcasted_iota(jnp.int32, (NB, NB), 0)
    col = lax.broadcasted_iota(jnp.int32, (NB, NB), 1)

    def panel(p, carried):
        at = pl.ds(pl.multiple_of(p * NB, NB), NB)
        done = unit_factor(work[at, at], STEP)
        pivots = jnp.sum(jnp.where(row == col, done, 0.0), axis=1, keepdims=True)
        unit = jnp.where(row > col, done, jnp.where(row == col, 1.0, 0.0))
        inv = unit * (1.0 / jnp.sqrt(pivots))
        below = lax.broadcasted_iota(jnp.int32, (n, NB), 0) >= (p + 1) * NB
        panel_col = jnp.where(below, contract_cols(work[:, at], inv), 0.0)
        work[...] = work[...] - contract_cols(panel_col, panel_col)
        out[at, :] = -matmul(inv, matmul(low[at, :], out[...]))
        out[at, at] = inv
        low[:, at] = panel_col
        return carried

    lax.fori_loop(0, n // NB, panel, 0)
    for b, (i, j) in enumerate(TRI):
        packed[b] = out[i * NB : i * NB + NB, j * NB : j * NB + NB]


def inverse_factor(gram):
    in_vmem = pl.BlockSpec(memory_space=pltpu.VMEM)
    return pl.pallas_call(
        inverse_factor_kernel,
        out_shape=[
            jax.ShapeDtypeStruct(gram.shape, jnp.float32),
            jax.ShapeDtypeStruct((len(TRI), NB, NB), jnp.float32),
        ],
        in_specs=[in_vmem],
        out_specs=[in_vmem, in_vmem],
        scratch_shapes=[pltpu.VMEM(gram.shape, jnp.float32)] * 2,
        name="inverse_factor",
    )(gram)


def class_sums_kernel(shifts, blocks, out):
    k = pl.program_id(0)

    @pl.when(k == 0)
    def _():
        out[...] = jnp.zeros_like(out)

    for i in range(blocks.shape[0]):
        c = shifts[k * blocks.shape[0] + i]
        out[c] = out[c] + blocks[i]


def class_sums(blocks, shifts):
    count, rows, width = blocks.shape
    per = 4
    return pl.pallas_call(
        class_sums_kernel,
        out_shape=jax.ShapeDtypeStruct((CLASSES, rows, width), jnp.float32),
        grid=(count // per,),
        in_specs=[pl.BlockSpec(memory_space=pltpu.SMEM), pl.BlockSpec((per, rows, width), lambda k: (k, 0, 0))],
        out_specs=pl.BlockSpec((CLASSES, rows, width), lambda k: (0, 0, 0)),
        name="class_sums",
    )(shifts, blocks)


def shifted(block, axis, distance):
    length = lax.axis_size(axis)
    return lax.ppermute(block, axis, [((i - distance) % length, i) for i in range(length)])


def sent_to_all(x, axis):
    length = lax.axis_size(axis)
    return lax.all_to_all(jnp.broadcast_to(x[None], (length, *x.shape)), axis, 0, 0, tiled=True)


def stacked_over(x, axis, dim):
    length = lax.axis_size(axis)
    here = lax.axis_index(axis)
    arrived = [x] + [shifted(x, axis, d) for d in range(1, length)]
    whole = jnp.zeros((*x.shape[:dim], length, *x.shape[dim:]), x.dtype)
    for d in range(length):
        whole = lax.dynamic_update_index_in_dim(whole, arrived[d], (here - d) % length, dim)
    return whole


def over_chips(z_rows):
    return stacked_over(z_rows, "op_0", 0).reshape(-1, z_rows.shape[-1])


def picked_kernel(shifts, blocks, out):
    for i in range(out.shape[0]):
        out[i] = blocks[shifts[pl.program_id(0) * out.shape[0] + i]]


def picked(blocks, shifts, per):
    inside = blocks.shape[1:]
    count = shifts.shape[0]
    zeros = (0,) * len(inside)
    return pl.pallas_call(
        picked_kernel,
        out_shape=jax.ShapeDtypeStruct((count, *inside), jnp.float32),
        grid=(count // per,),
        in_specs=[
            pl.BlockSpec(memory_space=pltpu.SMEM),
            pl.BlockSpec(blocks.shape, lambda k: (0, *zeros)),
        ],
        out_specs=pl.BlockSpec((per, *inside), lambda k: (k, *zeros)),
        name="picked",
    )(shifts, blocks)


def of_core(left_op):
    cut = left_op.reshape(left_op.shape[0], -1, 2, 32)
    here = lax.axis_index("op_2") == 0
    first, second = (cut[:, :, c].reshape(left_op.shape[0], -1) for c in range(2))
    return jnp.where(here, first, second), jnp.where(here, second, first)


def unpacked(blocks):
    blank = jnp.zeros((NB, NB), jnp.float32)
    rows = [[blocks[TRI.index((i, j))] if j <= i else blank for j in range(4)] for i in range(4)]
    return jnp.concatenate([jnp.concatenate(r, axis=1) for r in rows], axis=0)


def from_target(x, offset):
    for bit in (1, 0):
        arrived = shifted(x, SEC, -(1 << bit))
        x = jnp.where((offset >> bit) % 2 == 1, arrived, x)
    return x


def body(left_ops, right_ops, amplitudes, sketch, sector_shift):
    left_op = left_ops[0, 0]
    right_op = right_ops[0, 0]
    state = amplitudes[0]
    offset = sector_shift[0]
    shifts = sent_to_all(jnp.broadcast_to(sector_shift.astype(jnp.float32)[:, None], (1, 128)), OP)[:, 0, 0].astype(jnp.int32)
    left_here, left_there = of_core(left_op)
    state_here = over_chips(stacked_over(state, "op_1", 0))
    state_here, left_here, left_there = lax.optimization_barrier((state_here, left_here, left_there))
    state_there = shifted(state_here, "op_2", 1)
    term = matmul(left_here, matmul(state_here, right_op), CLOSE)
    term = term + matmul(left_there, matmul(state_there, right_op), CLOSE)
    term, late_state = lax.optimization_barrier((term, state))
    next_states = [late_state] + [shifted(late_state, SEC, -c) for c in range(1, CLASSES)]
    blocks = lax.all_to_all(term.reshape(32, -1, term.shape[-1]), OP, 0, 0, tiled=True)
    parts = class_sums(blocks, shifts)
    moved = [shifted(parts[c], SEC, c) for c in range(1, CLASSES)]
    correlation = sum(jnp.sum(next_states[c] * parts[c]) for c in range(CLASSES))
    partial = jnp.stack([correlation, jnp.sum(state * state)])
    totals = jnp.sum(sent_to_all(jnp.pad(partial, (0, 126))[None], OP_SEC), axis=(0, 1))
    energy = totals[0] / totals[1]
    sketched = matmul(parts[0] + sum(moved) - energy * state, sketch)
    here = over_chips(stacked_over(sketched, "op_1", 0))
    there = shifted(here, "op_2", 1)
    candidates = jnp.stack([sketched] + [shifted(sketched, SEC, -c) for c in range(1, CLASSES)])
    wanted, there = lax.optimization_barrier((picked(candidates, shifts, 8), there))
    inverse, triangle = inverse_factor(contract_rows(here, here) + contract_rows(there, there))
    target = lax.all_to_all(wanted, OP, 0, 0, tiled=True).reshape(-1, sketched.shape[-1])
    target_inverse = unpacked(from_target(triangle, offset))
    basis_slab = contract_cols(sketched, inverse)
    applied = matmul(left_here, contract_cols(here, inverse, CLOSE), CLOSE)
    applied = applied + matmul(left_there, contract_cols(there, inverse, CLOSE), CLOSE)
    rotated = matmul(target_inverse, contract_rows(target, applied, CLOSE), CLOSE)
    return (rotated[None, None], basis_slab[None], energy)


def solution(mesh):
    split = Mesh(mesh.devices.reshape(4, 4, 2, 4, 2), ("op_0", "op_1", "op_2", "sec_0", "sec_1"))
    in_specs = (P(OP, SEC, None, None), P(OP, SEC, None, None), P(SEC, OP, None), P(), P(OP))
    out_specs = (P(OP, SEC, None, None), P(SEC, OP, None), P())
    return jax.shard_map(body, mesh=split, in_specs=in_specs, out_specs=out_specs, check_vma=False)
```

```python
import jax
import jax.numpy as jnp
from jax import lax
from jax.experimental import pallas as pl
from jax.experimental.pallas import tpu as pltpu
from jax.sharding import Mesh
from jax.sharding import PartitionSpec as P

OP = ("op_0", "op_1", "op_2")
SEC = ("sec_0", "sec_1")
OP_SEC = ("op_0", "op_1", "op_2", "sec_0", "sec_1")
CLASSES = 4
NB = 128
STEP = 8
TRI = [(i, j) for i in range(4) for j in range(i + 1)]
EXACT = lax.Precision.HIGHEST
CLOSE = lax.Precision.HIGH


def dot(first, second, dims, precision=EXACT):
    return lax.dot_general(first, second, (dims, ((), ())), precision=precision, preferred_element_type=jnp.float32)


def matmul(first, second, precision=EXACT):
    return dot(first, second, ((1,), (0,)), precision)


def contract_rows(first, second, precision=EXACT):
    return dot(first, second, ((0,), (0,)), precision)


def contract_cols(first, second, precision=EXACT):
    return dot(first, second, ((1,), (1,)), precision)


def unit_factor(block, step):
    sub = lax.broadcasted_iota(jnp.int32, (8, NB), 0)
    lane = lax.broadcasted_iota(jnp.int32, (8, NB), 1)
    rows = [block[8 * r : 8 * r + 8] for r in range(NB // 8)]
    for start in range(0, NB, step):
        live = range(start // 8, NB // 8)
        cols = [{r: jnp.broadcast_to(rows[r][:, start + q : start + q + 1], (8, NB)) for r in live} for q in range(step)]
        for q in range(step):
            j = start + q
            at, inside = divmod(j, 8)
            one = slice(inside, inside + 1)
            inv = 1.0 / cols[q][at][one]
            line = jnp.broadcast_to(jnp.where(lane[:1] == j, 1.0, rows[at][one]) * inv, (8, NB))
            later = {p: jnp.broadcast_to(cols[p][at][one] * inv, (8, NB)) for p in range(q + 1, step)}
            for r in range(at, NB // 8):
                factor = cols[q][r]
                hit = lane == j
                if r == at:
                    factor = jnp.where(sub > inside, factor, 0.0)
                    hit = hit & (sub > inside)
                rows[r] = jnp.where(hit, 0.0, rows[r]) - factor * line
                for p in later:
                    cols[p][r] = cols[p][r] - factor * later[p]
    return jnp.concatenate(rows, axis=0)


def inverse_factor_kernel(gram, out, packed, work, low):
    n = gram.shape[0]
    work[...] = gram[...]
    low[...] = jnp.zeros_like(low)
    out[...] = jnp.zeros_like(out)
    row = lax.broadcasted_iota(jnp.int32, (NB, NB), 0)
    col = lax.broadcasted_iota(jnp.int32, (NB, NB), 1)

    def panel(p, carried):
        at = pl.ds(pl.multiple_of(p * NB, NB), NB)
        done = unit_factor(work[at, at], STEP)
        pivots = jnp.sum(jnp.where(row == col, done, 0.0), axis=1, keepdims=True)
        unit = jnp.where(row > col, done, jnp.where(row == col, 1.0, 0.0))
        inv = unit * (1.0 / jnp.sqrt(pivots))
        below = lax.broadcasted_iota(jnp.int32, (n, NB), 0) >= (p + 1) * NB
        panel_col = jnp.where(below, contract_cols(work[:, at], inv), 0.0)
        work[...] = work[...] - contract_cols(panel_col, panel_col)
        out[at, :] = -matmul(inv, matmul(low[at, :], out[...]))
        out[at, at] = inv
        low[:, at] = panel_col
        return carried

    lax.fori_loop(0, n // NB, panel, 0)
    for b, (i, j) in enumerate(TRI):
        packed[b] = out[i * NB : i * NB + NB, j * NB : j * NB + NB]


def inverse_factor(gram):
    in_vmem = pl.BlockSpec(memory_space=pltpu.VMEM)
    return pl.pallas_call(
        inverse_factor_kernel,
        out_shape=[
            jax.ShapeDtypeStruct(gram.shape, jnp.float32),
            jax.ShapeDtypeStruct((len(TRI), NB, NB), jnp.float32),
        ],
        in_specs=[in_vmem],
        out_specs=[in_vmem, in_vmem],
        scratch_shapes=[pltpu.VMEM(gram.shape, jnp.float32)] * 2,
        name="inverse_factor",
    )(gram)


def class_sums_kernel(shifts, blocks, out):
    k = pl.program_id(0)

    @pl.when(k == 0)
    def _():
        out[...] = jnp.zeros_like(out)

    for i in range(blocks.shape[0]):
        c = shifts[k * blocks.shape[0] + i]
        out[c] = out[c] + blocks[i]


def class_sums(blocks, shifts):
    count, rows, width = blocks.shape
    per = 4
    return pl.pallas_call(
        class_sums_kernel,
        out_shape=jax.ShapeDtypeStruct((CLASSES, rows, width), jnp.float32),
        grid=(count // per,),
        in_specs=[pl.BlockSpec(memory_space=pltpu.SMEM), pl.BlockSpec((per, rows, width), lambda k: (k, 0, 0))],
        out_specs=pl.BlockSpec((CLASSES, rows, width), lambda k: (0, 0, 0)),
        name="class_sums",
    )(shifts, blocks)


def shifted(block, axis, distance):
    length = lax.axis_size(axis)
    return lax.ppermute(block, axis, [((i - distance) % length, i) for i in range(length)])


def sent_to_all(x, axis):
    length = lax.axis_size(axis)
    return lax.all_to_all(jnp.broadcast_to(x[None], (length, *x.shape)), axis, 0, 0, tiled=True)


def sent_round(x, axis):
    return [x] + [shifted(x, axis, d) for d in range(1, lax.axis_size(axis))]


def stacked_over(x, axis, dim):
    return in_order(sent_round(x, axis), axis, dim)


def in_order(arrived, axis, dim):
    x = arrived[0]
    length = lax.axis_size(axis)
    here = lax.axis_index(axis)
    whole = jnp.zeros((*x.shape[:dim], length, *x.shape[dim:]), x.dtype)
    for d in range(length):
        whole = lax.dynamic_update_index_in_dim(whole, arrived[d], (here - d) % length, dim)
    return whole


def picked_kernel(shifts, blocks, out):
    for i in range(out.shape[0]):
        out[i] = blocks[shifts[pl.program_id(0) * out.shape[0] + i]]


def picked(blocks, shifts, per):
    inside = blocks.shape[1:]
    count = shifts.shape[0]
    zeros = (0,) * len(inside)
    return pl.pallas_call(
        picked_kernel,
        out_shape=jax.ShapeDtypeStruct((count, *inside), jnp.float32),
        grid=(count // per,),
        in_specs=[
            pl.BlockSpec(memory_space=pltpu.SMEM),
            pl.BlockSpec(blocks.shape, lambda k: (0, *zeros)),
        ],
        out_specs=pl.BlockSpec((per, *inside), lambda k: (k, *zeros)),
        name="picked",
    )(shifts, blocks)


def of_core(left_op, core):
    cut = left_op.reshape(left_op.shape[0], -1, 2, 32)
    here = core == 0
    first, second = (cut[:, :, c].reshape(left_op.shape[0], -1) for c in range(2))
    return jnp.concatenate([jnp.where(here, first, second), jnp.where(here, second, first)], axis=1)


def unpacked(blocks):
    blank = jnp.zeros((NB, NB), jnp.float32)
    rows = [[blocks[TRI.index((i, j))] if j <= i else blank for j in range(4)] for i in range(4)]
    return jnp.concatenate([jnp.concatenate(r, axis=1) for r in rows], axis=0)


def from_target(x, offset):
    for bit in (1, 0):
        arrived = shifted(x, SEC, -(1 << bit))
        x = jnp.where((offset >> bit) % 2 == 1, arrived, x)
    return x


def body(left_ops, right_ops, amplitudes, sketch, sector_shift):
    left_op = left_ops[0, 0]
    right_op = right_ops[0, 0]
    state = amplitudes[0]
    offset = sector_shift[0]
    shifts = sent_to_all(jnp.broadcast_to(sector_shift.astype(jnp.float32)[:, None], (1, 128)), OP)[:, 0, 0].astype(jnp.int32)
    arrived = sent_round(stacked_over(state, "op_1", 0), "op_0")
    left_op, arrived[1] = lax.optimization_barrier((left_op, arrived[1]))
    left_both = of_core(left_op, lax.axis_index("op_2"))
    state_here = in_order(arrived, "op_0", 0).reshape(-1, state.shape[-1])
    state_here, left_both = lax.optimization_barrier((state_here, left_both))
    state_there = shifted(state_here, "op_2", 1)
    right_part = jnp.concatenate([matmul(state_here, right_op, CLOSE), matmul(state_there, right_op, CLOSE)])
    term = matmul(left_both, right_part, CLOSE)
    term, late_state = lax.optimization_barrier((term, state))
    next_states = [late_state] + [shifted(late_state, SEC, -c) for c in range(1, CLASSES)]
    blocks = lax.all_to_all(term.reshape(32, -1, term.shape[-1]), OP, 0, 0, tiled=True)
    parts = class_sums(blocks, shifts)
    moved = [shifted(parts[c], SEC, c) for c in range(1, CLASSES)]
    correlation = sum(jnp.sum(next_states[c] * parts[c]) for c in range(CLASSES))
    partial = jnp.stack([correlation, jnp.sum(state * state)])
    totals = jnp.sum(sent_to_all(jnp.pad(partial, (0, 126))[None], OP_SEC), axis=(0, 1))
    energy = totals[0] / totals[1]
    sketched = matmul(parts[0] + sum(moved) - energy * state, sketch)
    arrived = sent_round(stacked_over(sketched, "op_1", 0), "op_0")
    late, arrived[1] = lax.optimization_barrier((sketched, arrived[1]))
    candidates = jnp.stack([late] + [shifted(late, SEC, -c) for c in range(1, CLASSES)])
    here = in_order(arrived, "op_0", 0).reshape(-1, sketched.shape[-1])
    here, candidates = lax.optimization_barrier((here, candidates))
    there = shifted(here, "op_2", 1)
    wanted, there = lax.optimization_barrier((picked(candidates, shifts, 8), there))
    rows = jnp.concatenate([here, there])
    inverse, triangle = inverse_factor(contract_rows(rows, rows))
    target = lax.all_to_all(wanted, OP, 0, 0, tiled=True).reshape(-1, sketched.shape[-1])
    target_inverse = unpacked(from_target(triangle, offset))
    basis_slab = contract_cols(sketched, inverse)
    applied = matmul(left_both, contract_cols(rows, inverse, CLOSE), CLOSE)
    rotated = matmul(target_inverse, contract_rows(target, applied, CLOSE), CLOSE)
    return (rotated[None, None], basis_slab[None], energy)


def solution(mesh):
    split = Mesh(mesh.devices.reshape(4, 4, 2, 4, 2), ("op_0", "op_1", "op_2", "sec_0", "sec_1"))
    in_specs = (P(OP, SEC, None, None), P(OP, SEC, None, None), P(SEC, OP, None), P(), P(OP))
    out_specs = (P(OP, SEC, None, None), P(SEC, OP, None), P())
    return jax.shard_map(body, mesh=split, in_specs=in_specs, out_specs=out_specs, check_vma=False)
```
